32 devices in a mesh: dp: 4 (over y, x), tensor: 4 (over z), pipe: 2 (over core).
Axes of the slice: x: 2, y: 2, z: 4, core: 2. Of those that a mesh axis runs over, the one named last changes fastest.
Arguments:
- acts: bfloat16 [6144, 4096], P(('dp', 'pipe')), may hold values from -6 to 6
- grad_hidden: bfloat16 [6144, 14336], P(('dp', 'pipe'), 'tensor'), may hold values from -384 to 384
- token_count: int32 [8], P(('dp', 'pipe')), may hold values from 1 to 768, as said below
- hot_ids: int32 [4, 358], P('tensor'), may hold values from 0 to 3583, as said below
- block_owner: int32 [112, 1], P('tensor'), may hold values from 0 to 3; in each aligned block of 28 rows (0 to 27, 28 to 55, ...) at most 14 rows name the same one
- master_hot: float32 [1432, 4096], P('tensor', ('dp', 'pipe')), may hold values from -6 to 6
- moment_hot: float32 [1432, 4096], P('tensor', ('dp', 'pipe')), may hold values from -3 to 3
- second_hot: float32 [1432, 4096], P('tensor', ('dp', 'pipe')), may hold values from 0.1 to 100
Outputs:
- new_master: float32 [1432, 4096], P('tensor', ('dp', 'pipe'))
- new_moment: float32 [1432, 4096], P('tensor', ('dp', 'pipe'))
- new_second: float32 [1432, 4096], P('tensor', ('dp', 'pipe'))
- hot_weights: bfloat16 [1432, 4096], P('tensor', 'dp')
- cold_sectioning: bfloat16 [224, 4096, 128], P('tensor', ('dp', 'pipe'))
The draws below stay inside these ranges and needn't reach their ends.
Inputs may be any that keep to these rules, and one draw needn't show every extreme that they name: `token_count`: each micro-batch has at least one live token, and some micro-batch has exactly 768. `hot_ids`: each row lists 358 different offsets. `block_owner`: within the 28 blocks of one tensor index, no owner is named more than 14 times.
All inputs are finite; a program needn't handle non-finite values.
Results may differ from the reference program's by a relative error of at most 0.015.
Values may be sent and summed in bfloat16 or wider, within the bound.
A program may use at most 128 MiB of HBM per device.

```python
import math
import jax
import jax.numpy as jnp
import numpy as np
from jax import lax

D = 4096
FF = 14336
TOK_DEV = 768
CB = 128
GROUPS = 8
TOKENS = 6144
FFS = 3584
HOT_TP = 358
HOT = 1432
BLOCKS = 28
SLOTS = 14
N_TENSOR = 4


def draw_token_count(key, part):
    index = jnp.arange(GROUPS, dtype=jnp.int32)
    low = TOK_DEV // 4
    base = low + (TOK_DEV - low) * index // max(GROUPS - 1, 1)
    jitter = jax.random.randint(jax.random.fold_in(key, 5), (GROUPS,), 0, max(TOK_DEV // 8, 1) + 1)
    jitter = jnp.where(index == GROUPS - 1, 0, jitter)
    return jnp.maximum(base - jitter, 1).astype(jnp.int32)


def draw_hot_ids(key, part):
    keys = jax.random.split(jax.random.fold_in(key, 17), N_TENSOR)

    def choose(single):
        return jax.random.permutation(single, FFS)[:HOT_TP]
    return jax.vmap(choose)(keys).astype(jnp.int32)


def block_levels(key, extent, cuts, smallest, top_value):
    def one(axis_at, blocks):
        heights = jax.random.uniform(jax.random.fold_in(jax.random.fold_in(key, 6), axis_at), (blocks,), jnp.float32, smallest / len(cuts), top_value / len(cuts))
        return jnp.repeat(jnp.exp(heights), extent[axis_at] // blocks).reshape((-1,) + (1,) * (len(extent) - axis_at - 1))

    loudness = one(*cuts[0])
    for cut in cuts[1:]:
        loudness = loudness * one(*cut)
    return loudness


def routed_block(own_key, own, number, rows, amount, top, most, slope):
    sequence = jax.random.permutation(own_key, amount)
    heavy_load, usual = load_shares(amount, rows * top, most, slope, True), load_shares(amount, rows * top, most, slope, False)
    places = jnp.arange(amount)

    def named(sizes, offset_by):
        used = int((sizes > 0).sum())
        fixed = max(1, used // 4)
        passed = fixed + (places - fixed + offset_by * (used - fixed)) % max(1, amount - fixed)
        return jnp.zeros((amount,), jnp.int32).at[sequence[jnp.where(places < fixed, places, passed)]].set(jnp.asarray(sizes, jnp.int32))

    sizes = jnp.where(number % 4 == 0, named(heavy_load, number // 4), named(usual, number - number // 4 - 1))
    mixed = jax.random.permutation(jax.random.fold_in(own, 3), amount)
    donor, receiver = mixed[0:amount // 2 * 2:2], mixed[1:amount // 2 * 2:2]
    room = jnp.minimum(sizes[donor] - 1, most - sizes[receiver]) // 2
    room = jnp.where((donor == sequence[0]) | (receiver == sequence[0]) | (sizes[receiver] == 0), 0, jnp.maximum(room, 0))
    passed = jax.random.randint(jax.random.fold_in(own, 4), (amount // 2,), 0, 1 << 20) % (room + 1)
    sizes = sizes.at[donor].add(-passed).at[receiver].add(passed)
    members = jnp.searchsorted(jnp.cumsum(sizes), jnp.arange(rows * top), side="right").astype(jnp.int32)
    listing = members.reshape(top, rows).T
    listing = listing[jax.random.permutation(jax.random.fold_in(own, 1), rows)]
    offset_by = jax.random.randint(jax.random.fold_in(own, 2), (rows, 1), 0, top)
    return jnp.take_along_axis(listing, (jnp.arange(top)[None, :] + offset_by) % top, axis=1)


def load_shares(count, total, reach, lean, full):
    loads = [(1 << 20) // math.isqrt(standing ** lean) + 1 for standing in range(1, count + 1)]
    largest = reach if full else min(reach, max(-(-total // count), total * loads[0] // sum(loads)))
    least = 1 if total - largest >= count - 1 else 0
    counts, rest = [largest] + [least] * (count - 1), total - largest - least * (count - 1)
    while rest > 0:
        candidates = [i for i in range(1, count) if counts[i] < largest] or [i for i in range(1, count) if counts[i] < reach]
        whole, budget = sum([loads[i] for i in candidates]), rest
        for i in candidates:
            extra = min(reach - counts[i], max(1, budget * loads[i] // whole), rest)
            counts[i] = counts[i] + extra
            rest = rest - extra
    return np.array(counts)


def normal_values(own_key, shape, spread, limit, cuts=(), kind=jnp.bfloat16):
    values = spread * jax.random.normal(own_key, shape, jnp.float32)
    if cuts:
        values = values * block_levels(own_key, shape, cuts, -0.22, 0.18)
    return jnp.clip(values, -limit, limit).astype(kind)


def setup_inputs(seed: int = 0) -> dict:
    key_list = jax.random.split(jax.random.key(seed), 9)
    acts = normal_values(key_list[0], (TOKENS, D), 1.0, 6.0, ((0, 8),))
    grad_hidden = normal_values(key_list[1], (TOKENS, FF), 64.0, 384.0, ((0, 8), (1, 4)))
    token_count = draw_token_count(jax.random.fold_in(key_list[8], 71), 0)
    hot_ids = draw_hot_ids(jax.random.fold_in(key_list[8], 71), 0)
    block_owner_keys = jax.random.split(jax.random.fold_in(key_list[4], 1), (N_TENSOR * BLOCKS) // BLOCKS)
    block_owner_turns = jax.random.permutation(jax.random.fold_in(key_list[4], 3), (N_TENSOR * BLOCKS) // BLOCKS)
    block_owner = jax.vmap(lambda own, number: routed_block(jax.random.fold_in(key_list[4], 2), own, number, BLOCKS, N_TENSOR, 1, SLOTS, 2))(block_owner_keys, block_owner_turns).reshape((N_TENSOR * BLOCKS, 1))
    master_hot = normal_values(key_list[5], (HOT, D), 1.0, 6.0, ((0, 4), (1, 8)), jnp.float32)
    moment_hot = normal_values(key_list[6], (HOT, D), 0.5, 3.0, ((0, 4), (1, 8)), jnp.float32)
    second_hot = jnp.clip(jnp.exp(math.log(100.0) - 6.9077553 * jax.random.uniform(key_list[7], (HOT, D), jnp.float32) ** block_levels(key_list[7], (HOT, D), ((0, 4), (1, 8)), -0.2, 0.2)), 0.1, 100.0)
    return {"acts": acts, "grad_hidden": grad_hidden, "token_count": token_count, "hot_ids": hot_ids, "block_owner": block_owner, "master_hot": master_hot, "moment_hot": moment_hot, "second_hot": second_hot}


def reference(acts, grad_hidden, token_count, hot_ids, block_owner, master_hot, moment_hot, second_hot):
    slot_pos = jnp.arange(TOKENS, dtype=jnp.int32) % TOK_DEV
    live = slot_pos < jnp.repeat(token_count, TOK_DEV)
    masked = jnp.where(live[:, None], grad_hidden, jnp.zeros_like(grad_hidden))
    total = jnp.sum(token_count.astype(jnp.float32))
    inputs = acts.reshape(GROUPS, TOK_DEV, D)
    outputs = masked.reshape(GROUPS, TOK_DEV, FF)

    def accumulate(carry, pair):
        left, right = pair
        partial_value = jnp.dot(left.T, right, preferred_element_type=jnp.float32).astype(jnp.bfloat16)
        partial_value = lax.optimization_barrier(partial_value)
        return (carry + partial_value.astype(jnp.float32), None)
    summed, _ = lax.scan(accumulate, jnp.zeros((D, FF), jnp.float32), (inputs, outputs))
    grad = summed / total
    hot_cols = (jnp.arange(N_TENSOR, dtype=jnp.int32)[:, None] * FFS + hot_ids).reshape(HOT).astype(jnp.int32)
    g_hot = grad[:, hot_cols].T
    new_moment = 0.9 * moment_hot + 0.1 * g_hot
    new_second = 0.95 * second_hot + 0.05 * g_hot * g_hot
    bias_one = 1.0 - 0.9 ** 4
    bias_two = 1.0 - 0.95 ** 4
    new_master = master_hot - 0.02 * (new_moment / bias_one) / (jnp.sqrt(new_second / bias_two) + 1e-08)
    hot_weights = new_master.astype(jnp.bfloat16)
    is_hot = jnp.zeros((FF,), jnp.bool_).at[hot_cols].set(True)
    cold = jnp.where(is_hot[None, :], 0.0, grad).astype(jnp.bfloat16)
    blocks = cold.reshape(D, N_TENSOR, BLOCKS, CB).transpose(1, 2, 0, 3)
    owner = block_owner.reshape(N_TENSOR, BLOCKS)
    same = owner[:, :, None] == owner[:, None, :]
    index = jnp.arange(BLOCKS, dtype=jnp.int32)
    earlier = index[None, :] < index[:, None]
    slot = lax.optimization_barrier(jnp.sum((same & earlier[None, :, :]).astype(jnp.int32), axis=2))
    source = jnp.arange(N_TENSOR, dtype=jnp.int32)[:, None]
    target = ((owner * N_TENSOR + source) * SLOTS + slot).reshape(-1).astype(jnp.int32)
    sectioning = jnp.zeros((N_TENSOR * N_TENSOR * SLOTS, D, CB), jnp.bfloat16)
    cold_sectioning = sectioning.at[target].set(blocks.reshape(N_TENSOR * BLOCKS, D, CB))
    return (new_master, new_moment, new_second, hot_weights, cold_sectioning)
```

```python
import functools

import jax
import jax.numpy as jnp
from jax import lax
from jax.experimental import pallas as pl
from jax.experimental.pallas import tpu as pltpu
from jax.sharding import PartitionSpec as P

CB = 128
GROUP = 8
LAGS = (1, 2, 2)


def fused(
    sizes, tc_ref, place_ref, hid_ref, acts, gh, mst, mom, sec,
    mst_out, mom_out, sec_out, hw_out, cs_out,
    acts_v, gh_v, acts_t, select, keep, hot_acc, state, hw_v, slots_v,
    recv_a, recv_b, recv_c, tiles, packed, count,
    acts_sem, gh_sem, state_sem, count_sem, send_a, land_a, send_b, land_b, send_c, land_c,
    z_send, z_land, hw_sem,
):
    chunks, pieces, w, tensors, slots, width = sizes
    half = CB // 2
    total_pieces = chunks * pieces
    ring = slots_v.shape[0]
    row_count = chunks * CB
    lag_b = LAGS[0]
    lag_c = lag_b + LAGS[1]
    lag_d = lag_c + LAGS[2]
    dp, tz, pp = lax.axis_index("dp"), lax.axis_index("tensor"), lax.axis_index("pipe")
    y, x = dp // 2, dp % 2

    def peer(qy, qx, qc):
        return (((y + qy) % 2) * 2 + (x + qx) % 2, tz, (pp + qc) % 2)

    def remote(src, dst, ssem, rsem, device):
        return pltpu.make_async_remote_copy(
            src_ref=src, dst_ref=dst, send_sem=ssem, recv_sem=rsem,
            device_id=device, device_id_type=pl.DeviceIdType.MESH,
        )

    def acts_copy(c, o):
        return pltpu.make_async_copy(
            acts.at[:, pl.ds(pl.multiple_of(o * row_count + c * CB, CB), CB)],
            acts_v.at[c, o], acts_sem.at[c, o],
        )

    def gh_copy(p):
        return pltpu.make_async_copy(
            gh.at[:, pl.ds(pl.multiple_of(p * w, CB), w)], gh_v.at[p], gh_sem.at[p]
        )

    state_in = [
        pltpu.make_async_copy(r, state.at[k], state_sem.at[k])
        for k, r in enumerate((mst, mom, sec))
    ]
    for o in range(GROUP):
        acts_copy(0, o).start()
    gh_copy(0).start()
    for p in range(1, pieces):
        gh_copy(p).start()
    for c in range(1, chunks):
        for o in range(GROUP):
            acts_copy(c, o).start()
    for cp in state_in:
        cp.start()

    count[0] = jnp.full((8, 128), tc_ref[0], jnp.int32).astype(jnp.float32)
    barrier = pltpu.get_barrier_semaphore()
    for q in range(1, GROUP):
        pl.semaphore_signal(
            barrier, inc=1, device_id=peer(q // 4, (q // 2) % 2, q % 2),
            device_id_type=pl.DeviceIdType.MESH,
        )
    for d in range(1, tensors):
        pl.semaphore_signal(
            barrier, inc=1, device_id=(dp, (tz + d) % tensors, pp),
            device_id_type=pl.DeviceIdType.MESH,
        )
    pl.semaphore_wait(barrier, GROUP - 1 + tensors - 1)

    counts = [
        remote(
            count.at[0], count.at[q], count_sem.at[0, q], count_sem.at[1, q],
            peer(q // 4, (q // 2) % 2, q % 2),
        )
        for q in range(1, GROUP)
    ]
    for cp in counts:
        cp.start()

    def copy_a(i, h):
        return remote(
            slots_v.at[i % ring, h, pl.ds(4, 4)], recv_a.at[i, h],
            send_a.at[i, h], land_a.at[i, h], peer(0, 0, 1),
        )

    def copy_b(i, h):
        return remote(
            slots_v.at[i % ring, h, pl.ds(2, 2)], recv_b.at[i, h],
            send_b.at[i, h], land_b.at[i, h], peer(h, 1 - h, 0),
        )

    def copy_c(i, h):
        return remote(
            slots_v.at[i % ring, h, 1], recv_c.at[i, h],
            send_c.at[i, h], land_c.at[i, h], peer(1 - h, h, 0),
        )

    def z_copy(c, d):
        return remote(
            packed.at[c, pl.ds(((tz + d) % tensors) * slots, slots)],
            cs_out.at[pl.ds(tz * slots, slots), pl.ds(c * CB, CB)],
            z_send.at[c, d], z_land.at[c, d], (dp, (tz + d) % tensors, pp),
        )

    def z_own(c):
        return pltpu.make_async_copy(
            packed.at[c, pl.ds(tz * slots, slots)],
            cs_out.at[pl.ds(tz * slots, slots), pl.ds(c * CB, CB)],
            z_send.at[c, 0],
        )

    tok = acts_v.shape[2]
    live = lax.broadcasted_iota(jnp.int32, (tok, CB), 0) < tc_ref[0]
    tiles[tiles.shape[0] - 1] = jnp.zeros((CB, CB), tiles.dtype)

    def multiply(i):
        c, p = i // pieces, i % pieces

        @pl.when(p == 0)
        def _():
            for o in range(GROUP):
                acts_copy(c, o).wait()
            for q in range(GROUP):
                qc, q1, q0 = q // 4, (q // 2) % 2, q % 2
                o = ((y + q0) % 2) * 4 + ((x + q1) % 2) * 2 + (pp + qc) % 2
                v = jnp.where(live, acts_v[c, o].astype(jnp.float32), 0.0)
                acts_t[pl.ds(q * CB, CB)] = v.T.astype(jnp.bfloat16)

        @pl.when(c == 0)
        def _():
            gh_copy(p).wait()

        def halfway(k, carry):
            base = pl.multiple_of(k * 4 * CB, CB)
            r = jnp.dot(
                acts_t[pl.ds(base, 4 * CB)], gh_v[p], preferred_element_type=jnp.float32
            ).astype(jnp.bfloat16)
            for q in range(4):
                a, b = q % 2, q // 2
                slots_v[i % ring, 0, k * 4 + q] = r[q * CB : q * CB + half]
                slots_v[i % ring, 1, k * 4 + a * 2 + b] = r[q * CB + half : (q + 1) * CB]
            return carry

        lax.fori_loop(0, 2, halfway, 0)
        for h in range(2):
            copy_a(i, h).start()

    def prepare():
        for p in range(pieces):
            column = lax.broadcasted_iota(jnp.int32, (select.shape[1], w), 1) + p * w
            hit = (column == hid_ref[...]).astype(jnp.float32)
            select[p] = hit.astype(jnp.bfloat16)
            keep[p] = jnp.broadcast_to(1.0 - jnp.max(hit, axis=0, keepdims=True), (8, w))
        for cp in counts:
            cp.wait()
        for cp in state_in:
            cp.wait()

    f32 = jnp.float32

    def step_b(i):
        for h in range(2):
            copy_a(i, h).wait()
            for k in (2, 3, 0, 1):
                slots_v[i % ring, h, k] = (
                    slots_v[i % ring, h, k].astype(f32) + recv_a[i, h, k].astype(f32)
                ).astype(jnp.bfloat16)
            copy_b(i, h).start()

    def step_c(i):
        for h in range(2):
            copy_b(i, h).wait()
            for k in (1, 0):
                slots_v[i % ring, h, k] = (
                    slots_v[i % ring, h, k].astype(f32) + recv_b[i, h, k].astype(f32)
                ).astype(jnp.bfloat16)
            copy_c(i, h).start()

    def step_d(i):
        c, p = i // pieces, i % pieces
        total = count[0]
        for q in range(1, GROUP):
            total = total + count[q]
        total = total[0:1, 0:1]
        parts = []
        for h in range(2):
            copy_c(i, h).wait()
            s = slots_v[i % ring, h, 0].astype(f32) + recv_c[i, h].astype(f32)
            cold = jnp.where(keep[p][0:1] > 0.5, s / total, 0.0).astype(jnp.bfloat16)
            for b in range(w // CB):
                tiles[p * (w // CB) + b, pl.ds(h * half, half)] = cold[:, b * CB : (b + 1) * CB]
            parts.append(s.astype(jnp.bfloat16))
        whole = jnp.concatenate(parts, axis=0)
        g = lax.dot_general(
            select[p], whole, (((1,), (1,)), ((), ())), preferred_element_type=f32
        )

        @pl.when(p == 0)
        def _():
            hot_acc[...] = g

        @pl.when(p > 0)
        def _():
            hot_acc[...] = hot_acc[...] + g

        @pl.when(p == pieces - 1)
        def _():
            def place(k, carry):
                packed[c, k] = tiles[place_ref[k]]
                return carry

            lax.fori_loop(0, tensors * slots, place, 0)
            for d in range(tensors - 1, 0, -1):
                z_copy(c, d).start()
            z_own(c).start()
            cols = pl.ds(pl.multiple_of(c * CB, CB), CB)
            out = adam_update(
                hot_acc[...] / total, state[0, :, cols], state[1, :, cols], state[2, :, cols]
            )
            for k in range(3):
                state[k, :, cols] = out[k]
            hw_v[:, cols] = out[0].astype(jnp.bfloat16)

    def body(i, carry):
        @pl.when(i < total_pieces)
        def _():
            multiply(i)

        @pl.when(i == 1)
        def _():
            prepare()

        @pl.when((i >= lag_d) & (i < total_pieces + lag_d))
        def _():
            step_d(i - lag_d)

        @pl.when((i >= lag_c) & (i < total_pieces + lag_c))
        def _():
            step_c(i - lag_c)

        @pl.when((i >= lag_b) & (i < total_pieces + lag_b))
        def _():
            step_b(i - lag_b)

        return carry

    lax.fori_loop(0, total_pieces + lag_d, body, 0)

    mine = hw_out.at[:, pl.ds(pl.multiple_of(pp * row_count, CB), row_count)]
    swap = remote(hw_v, mine, hw_sem.at[0], hw_sem.at[1], peer(0, 0, 1))
    swap.start()
    outs = [
        pltpu.make_async_copy(state.at[k], r, state_sem.at[k])
        for k, r in enumerate((mst_out, mom_out, sec_out))
    ]
    outs.append(pltpu.make_async_copy(hw_v, mine, hw_sem.at[2]))
    for cp in outs:
        cp.start()
    for cp in outs:
        cp.wait()
    swap.wait()
    for c in range(chunks):
        z_own(c).wait()
        for d in range(tensors - 1, 0, -1):
            z_copy(c, d).wait()


def fused_call(tok, placing, hot_ids, acts, grad_hidden, master, moment, second, slots):
    tensors = lax.axis_size("tensor")
    t, width = grad_hidden.shape
    hot, rows = master.shape
    chunks = rows // CB
    blocks = width // CB
    per = 4 if blocks % 4 == 0 else 1
    w = per * CB
    pieces = blocks // per
    n = chunks * pieces
    half = CB // 2
    bf16, f32 = jnp.bfloat16, jnp.float32
    dma = pltpu.SemaphoreType.DMA
    hbm = pl.BlockSpec(memory_space=pl.ANY)
    smem = pl.BlockSpec(memory_space=pltpu.SMEM)
    state = jax.ShapeDtypeStruct((hot, rows), f32)
    return pl.pallas_call(
        functools.partial(fused, (chunks, pieces, w, tensors, slots, width)),
        out_shape=(
            state, state, state,
            jax.ShapeDtypeStruct((hot, 2 * rows), bf16),
            jax.ShapeDtypeStruct((tensors * slots, rows, CB), bf16),
        ),
        in_specs=[smem, smem, pl.BlockSpec(memory_space=pltpu.VMEM)] + [hbm] * 5,
        out_specs=(hbm,) * 5,
        scratch_shapes=[
            pltpu.VMEM((chunks, GROUP, t, CB), bf16),
            pltpu.VMEM((pieces, t, w), bf16),
            pltpu.VMEM((GROUP * CB, t), bf16),
            pltpu.VMEM((pieces, hot, w), bf16),
            pltpu.VMEM((pieces, 8, w), f32),
            pltpu.VMEM((hot, CB), f32),
            pltpu.VMEM((3, hot, rows), f32),
            pltpu.VMEM((hot, rows), bf16),
            pltpu.VMEM((sum(LAGS) + 1, 2, GROUP, half, w), bf16),
            pltpu.VMEM((n, 2, 4, half, w), bf16),
            pltpu.VMEM((n, 2, 2, half, w), bf16),
            pltpu.VMEM((n, 2, half, w), bf16),
            pltpu.VMEM((blocks + 1, CB, CB), bf16),
            pltpu.VMEM((chunks, tensors * slots, CB, CB), bf16),
            pltpu.VMEM((GROUP, 8, 128), f32),
            dma((chunks, GROUP)), dma((pieces,)), dma((3,)), dma((2, GROUP)),
            dma((n, 2)), dma((n, 2)), dma((n, 2)), dma((n, 2)), dma((n, 2)), dma((n, 2)),
            dma((chunks, tensors)), dma((chunks, tensors)), dma((3,)),
        ],
        compiler_params=pltpu.CompilerParams(
            collective_id=0, has_side_effects=True, vmem_limit_bytes=67043328
        ),
    )(tok, placing, hot_ids, acts, grad_hidden, master, moment, second)


def adam_update(g_hot, master_hot, moment_hot, second_hot):
    new_moment = 0.9 * moment_hot + 0.1 * g_hot
    new_second = 0.95 * second_hot + 0.05 * g_hot * g_hot
    bias_one = 1.0 - 0.9**4
    bias_two = 1.0 - 0.95**4
    new_master = master_hot - 0.02 * (new_moment / bias_one) / (
        jnp.sqrt(new_second / bias_two) + 1e-08
    )
    return (new_master, new_moment, new_second)


def shards(
    acts, grad_hidden, token_count, hot_ids, block_owner, master_hot, moment_hot, second_hot
):
    tok_slots = acts.shape[0]
    width = grad_hidden.shape[1]
    hot_count = hot_ids.shape[1]
    row_count = master_hot.shape[1]
    tensors = lax.axis_size("tensor")
    blocks = width // CB
    slots = max(2, (2 * blocks + tensors - 1) // tensors)
    if lax.axis_size("dp") == 4 and lax.axis_size("pipe") == 2 and row_count % CB == 0:
        owner = block_owner[:, 0]
        same = owner[:, None] == owner[None, :]
        index = lax.broadcasted_iota(jnp.int32, (blocks, blocks), 0)
        other = lax.broadcasted_iota(jnp.int32, (blocks, blocks), 1)
        slot = jnp.sum((same & (other < index)).astype(jnp.int32), axis=1)
        target = owner * slots + slot
        places = lax.broadcasted_iota(jnp.int32, (tensors * slots, blocks), 0)
        number = lax.broadcasted_iota(jnp.int32, (tensors * slots, blocks), 1)
        from_block = jnp.min(jnp.where(places == target[None, :], number, blocks), axis=1)
        return fused_call(
            token_count, from_block, hot_ids.reshape(hot_count, 1), acts, grad_hidden,
            master_hot, moment_hot, second_hot, slots,
        )
    live = lax.broadcasted_iota(jnp.int32, (tok_slots, 1), 0) < token_count[0]
    masked = jnp.where(live, grad_hidden, jnp.zeros_like(grad_hidden))
    total = lax.psum(token_count.astype(jnp.float32)[0], ("dp", "pipe"))
    column = lax.broadcasted_iota(jnp.int32, (width, hot_count), 0)
    selector = column == hot_ids[0][None, :]
    hot_mask = jnp.any(selector, axis=1)
    contract = (((0,), (0,)), ((), ()))
    summed = lax.psum_scatter(
        lax.dot_general(acts, masked, contract, preferred_element_type=jnp.float32).astype(
            jnp.bfloat16
        ),
        ("dp", "pipe"),
        scatter_dimension=0,
        tiled=True,
    ).astype(jnp.float32)
    grad = summed / total
    g_hot = lax.dot_general(
        selector.astype(jnp.float32),
        grad,
        (((0,), (1,)), ((), ())),
        precision=lax.Precision.HIGHEST,
        preferred_element_type=jnp.float32,
    )
    cold = jnp.where(hot_mask[None, :], 0.0, grad).astype(jnp.bfloat16)
    new_master, new_moment, new_second = adam_update(g_hot, master_hot, moment_hot, second_hot)
    hot_weights = lax.all_gather(new_master.astype(jnp.bfloat16), "pipe", axis=1, tiled=True)
    owner = block_owner[:, 0]
    same = owner[:, None] == owner[None, :]
    index = lax.broadcasted_iota(jnp.int32, (blocks, blocks), 0)
    other = lax.broadcasted_iota(jnp.int32, (blocks, blocks), 1)
    slot = jnp.sum((same & (other < index)).astype(jnp.int32), axis=1)
    target = owner * slots + slot
    places = lax.broadcasted_iota(jnp.int32, (tensors * slots, blocks), 0)
    placing = (places == target[None, :]).astype(jnp.bfloat16)
    tiles = cold.reshape(row_count, blocks, CB)
    packed = jnp.einsum("pb,rbc->prc", placing, tiles, preferred_element_type=jnp.float32).astype(
        jnp.bfloat16
    )
    cold_sectioning = lax.all_to_all(packed, "tensor", split_axis=0, concat_axis=0, tiled=True)
    return (new_master, new_moment, new_second, hot_weights, cold_sectioning)


def solution(mesh):
    in_specs = (
        P(("dp", "pipe"), None),
        P(("dp", "pipe"), "tensor"),
        P(("dp", "pipe")),
        P("tensor", None),
        P("tensor", None),
        P("tensor", ("dp", "pipe")),
        P("tensor", ("dp", "pipe")),
        P("tensor", ("dp", "pipe")),
    )
    out_specs = (
        P("tensor", ("dp", "pipe")),
        P("tensor", ("dp", "pipe")),
        P("tensor", ("dp", "pipe")),
        P("tensor", "dp"),
        P("tensor", ("dp", "pipe"), None),
    )
    return jax.shard_map(shards, mesh=mesh, in_specs=in_specs, out_specs=out_specs, check_vma=False)
```

```python
import functools

import jax
import jax.numpy as jnp
from jax import lax
from jax.experimental import pallas as pl
from jax.experimental.pallas import tpu as pltpu
from jax.sharding import PartitionSpec as P

CB = 128
GROUP = 8
ROWS = 64
PER = 7
LAGS = (1, 2, 2)


def fused(
    sizes, tc_ref, place_ref, hid_ref, acts, gh, mst, mom, sec,
    mst_out, mom_out, sec_out, hw_out, cs_out,
    acts_v, gh_v, acts_t, select, keep, hot_acc, state, hw_v, slots_v,
    recv_a, recv_b, recv_c, tiles, sums, packed, count,
    acts_sem, gh_sem, state_sem, count_sem, send_a, land_a, send_b, land_b, send_c, land_c,
    z_send, z_land, hw_sem,
):
    chunks, pieces, w, tensors, slots, width = sizes
    half = ROWS // 2
    total_pieces = chunks * pieces
    ring = slots_v.shape[0]
    row_count = chunks * ROWS
    lag_b = LAGS[0]
    lag_c = lag_b + LAGS[1]
    lag_d = lag_c + LAGS[2]
    dp, tz, pp = lax.axis_index("dp"), lax.axis_index("tensor"), lax.axis_index("pipe")
    y, x = dp // 2, dp % 2

    def peer(qy, qx, qc):
        return (((y + qy) % 2) * 2 + (x + qx) % 2, tz, (pp + qc) % 2)

    def remote(src, dst, ssem, rsem, device):
        return pltpu.make_async_remote_copy(
            src_ref=src, dst_ref=dst, send_sem=ssem, recv_sem=rsem,
            device_id=device, device_id_type=pl.DeviceIdType.MESH,
        )

    def acts_copy(c, o):
        return pltpu.make_async_copy(
            acts.at[:, pl.ds(pl.multiple_of(o * row_count + c * CB, CB), CB)],
            acts_v.at[c, o], acts_sem.at[c, o],
        )

    def gh_copy(p):
        return pltpu.make_async_copy(
            gh.at[:, pl.ds(pl.multiple_of(p * w, CB), w)], gh_v.at[p], gh_sem.at[p]
        )

    state_in = [
        pltpu.make_async_copy(r, state.at[k], state_sem.at[k])
        for k, r in enumerate((mst, mom, sec))
    ]
    for o in range(GROUP):
        acts_copy(0, o).start()
    gh_copy(0).start()
    for p in range(1, pieces):
        gh_copy(p).start()
    for c in range(1, row_count // CB):
        for o in range(GROUP):
            acts_copy(c, o).start()
    for cp in state_in:
        cp.start()

    count[0] = jnp.full((8, 128), tc_ref[0], jnp.int32).astype(jnp.float32)
    barrier = pltpu.get_barrier_semaphore()
    for q in range(1, GROUP):
        pl.semaphore_signal(
            barrier, inc=1, device_id=peer(q // 4, (q // 2) % 2, q % 2),
            device_id_type=pl.DeviceIdType.MESH,
        )
    for d in range(1, tensors):
        pl.semaphore_signal(
            barrier, inc=1, device_id=(dp, (tz + d) % tensors, pp),
            device_id_type=pl.DeviceIdType.MESH,
        )
    pl.semaphore_wait(barrier, GROUP - 1 + tensors - 1)

    counts = [
        remote(
            count.at[0], count.at[q], count_sem.at[0, q], count_sem.at[1, q],
            peer(q // 4, (q // 2) % 2, q % 2),
        )
        for q in range(1, GROUP)
    ]
    for cp in counts:
        cp.start()

    def copy_a(i, h):
        return remote(
            slots_v.at[i % ring, h, pl.ds(4, 4)], recv_a.at[i, h],
            send_a.at[i, h], land_a.at[i, h], peer(0, 0, 1),
        )

    def copy_b(i, h):
        return remote(
            slots_v.at[i % ring, h, pl.ds(2, 2)], recv_b.at[i, h],
            send_b.at[i, h], land_b.at[i, h], peer(h, 1 - h, 0),
        )

    def copy_c(i, h):
        return remote(
            slots_v.at[i % ring, h, 1], recv_c.at[i, h],
            send_c.at[i, h], land_c.at[i, h], peer(1 - h, h, 0),
        )

    def z_copy(c, d):
        return remote(
            packed.at[c, pl.ds(((tz + d) % tensors) * slots, slots)],
            cs_out.at[pl.ds(tz * slots, slots), pl.ds(c * ROWS, ROWS)],
            z_send.at[c, d], z_land.at[c, d], (dp, (tz + d) % tensors, pp),
        )

    def z_own(c):
        return pltpu.make_async_copy(
            packed.at[c, pl.ds(tz * slots, slots)],
            cs_out.at[pl.ds(tz * slots, slots), pl.ds(c * ROWS, ROWS)],
            z_send.at[c, 0],
        )

    tok = acts_v.shape[2]
    live = lax.broadcasted_iota(jnp.int32, (tok, CB), 0) < tc_ref[0]
    hot_acc[...] = jnp.zeros_like(hot_acc)
    tiles[tiles.shape[0] - 1] = jnp.zeros((ROWS, CB), tiles.dtype)

    def multiply(i):
        c, p = i // pieces, i % pieces

        @pl.when((p == 0) & (c % 2 == 0))
        def _():
            for o in range(GROUP):
                acts_copy(c // 2, o).wait()
            for q in range(GROUP):
                qc, q1, q0 = q // 4, (q // 2) % 2, q % 2
                o = ((y + q0) % 2) * 4 + ((x + q1) % 2) * 2 + (pp + qc) % 2
                v = jnp.where(live, acts_v[c // 2, o].astype(jnp.float32), 0.0)
                v = v.T.astype(jnp.bfloat16)
                acts_t[0, pl.ds(q * ROWS, ROWS)] = v[:ROWS]
                acts_t[1, pl.ds(q * ROWS, ROWS)] = v[ROWS:]

        @pl.when(c == 0)
        def _():
            gh_copy(p).wait()

        r = jnp.dot(
            acts_t[c % 2], gh_v[p], preferred_element_type=jnp.float32
        ).astype(jnp.bfloat16)
        for q in range(GROUP):
            k, a, b = q // 4, q % 2, (q // 2) % 2
            slots_v[i % ring, 0, q] = r[q * ROWS : q * ROWS + half]
            slots_v[i % ring, 1, k * 4 + a * 2 + b] = r[q * ROWS + half : (q + 1) * ROWS]
        for h in range(2):
            copy_a(i, h).start()

    def prepare():
        for p in range(pieces):
            column = lax.broadcasted_iota(jnp.int32, (select.shape[1], w), 1) + p * w
            hit = (column == hid_ref[...]).astype(jnp.float32)
            select[p] = hit.astype(jnp.bfloat16)
            keep[p] = jnp.broadcast_to(1.0 - jnp.max(hit, axis=0, keepdims=True), (8, w))
        for cp in counts:
            cp.wait()
        for cp in state_in:
            cp.wait()

    f32 = jnp.float32

    def step_b(i):
        for h in range(2):
            copy_a(i, h).wait()
            for k in (2, 3, 0, 1):
                slots_v[i % ring, h, k] = (
                    slots_v[i % ring, h, k].astype(f32) + recv_a[i, h, k].astype(f32)
                ).astype(jnp.bfloat16)
            copy_b(i, h).start()

    def step_c(i):
        for h in range(2):
            copy_b(i, h).wait()
            for k in (1, 0):
                slots_v[i % ring, h, k] = (
                    slots_v[i % ring, h, k].astype(f32) + recv_b[i, h, k].astype(f32)
                ).astype(jnp.bfloat16)
            copy_c(i, h).start()

    def step_d(i):
        c, p = i // pieces, i % pieces
        total = count[0]
        for q in range(1, GROUP):
            total = total + count[q]
        total = total[0:1, 0:1]
        for h in range(2):
            copy_c(i, h).wait()
            s = slots_v[i % ring, h, 0].astype(f32) + recv_c[i, h].astype(f32)
            cold = jnp.where(keep[p][0:1] > 0.5, s / total, 0.0).astype(jnp.bfloat16)
            for b in range(w // CB):
                tiles[p * (w // CB) + b, pl.ds(h * half, half)] = cold[:, b * CB : (b + 1) * CB]
            sums[p, pl.ds((c % 2) * ROWS + h * half, half)] = s.astype(jnp.bfloat16)

        @pl.when(c % 2 == 1)
        def _():
            g = lax.dot_general(
                select[p], sums[p], (((1,), (1,)), ((), ())), preferred_element_type=f32
            )
            hot_acc[...] = jnp.where(p == 0, 0.0, hot_acc[...]) + g

        @pl.when(p == pieces - 1)
        def _():
            def place(k, carry):
                packed[c, k] = tiles[place_ref[k]]
                return carry

            lax.fori_loop(0, tensors * slots, place, 0)
            for d in range(tensors - 1, 0, -1):
                z_copy(c, d).start()
            z_own(c).start()

        @pl.when((p == pieces - 1) & (c % 2 == 1))
        def _():
            cols = pl.ds(pl.multiple_of((c // 2) * CB, CB), CB)
            out = adam_update(
                hot_acc[...] / total, state[0, :, cols], state[1, :, cols], state[2, :, cols]
            )
            for k in range(3):
                state[k, :, cols] = out[k]
            hw_v[:, cols] = out[0].astype(jnp.bfloat16)

    def body(i, carry):
        @pl.when(i < total_pieces)
        def _():
            multiply(i)

        @pl.when(i == 1)
        def _():
            prepare()

        @pl.when((i >= lag_d) & (i < total_pieces + lag_d))
        def _():
            step_d(i - lag_d)

        @pl.when((i >= lag_c) & (i < total_pieces + lag_c))
        def _():
            step_c(i - lag_c)

        @pl.when((i >= lag_b) & (i < total_pieces + lag_b))
        def _():
            step_b(i - lag_b)

        return carry

    lax.fori_loop(0, total_pieces + lag_d, body, 0)

    mine = hw_out.at[:, pl.ds(pl.multiple_of(pp * row_count, CB), row_count)]
    swap = remote(hw_v, mine, hw_sem.at[0], hw_sem.at[1], peer(0, 0, 1))
    swap.start()
    outs = [
        pltpu.make_async_copy(state.at[k], r, state_sem.at[k])
        for k, r in enumerate((mst_out, mom_out, sec_out))
    ]
    outs.append(pltpu.make_async_copy(hw_v, mine, hw_sem.at[2]))
    for cp in outs:
        cp.start()
    for cp in outs:
        cp.wait()
    swap.wait()
    for c in range(chunks):
        z_own(c).wait()
        for d in range(tensors - 1, 0, -1):
            z_copy(c, d).wait()


def hand_out(refs, outs, bufs, sems, splits):
    jobs = []
    for k in range(len(splits)):
        size = bufs[k].shape[0] // splits[k]
        for j in range(splits[k]):
            part = pl.ds(j * size, size)
            jobs.append((
                pltpu.make_async_copy(refs[k].at[part], bufs[k].at[part], sems[k].at[0, j]),
                pltpu.make_async_copy(bufs[k].at[part], outs[k].at[part], sems[k].at[1, j]),
            ))
    for load, _ in jobs:
        load.start()
    for load, store in jobs:
        load.wait()
        store.start()
    for _, store in jobs:
        store.wait()


def hand_out_call(arrays, splits):
    n = len(arrays)
    hbm = pl.BlockSpec(memory_space=pl.ANY)

    def kernel(*refs):
        hand_out(refs[:n], refs[n : 2 * n], refs[2 * n : 3 * n], refs[3 * n :], splits)

    return pl.pallas_call(
        kernel,
        out_shape=tuple(jax.ShapeDtypeStruct(a.shape, a.dtype) for a in arrays),
        in_specs=[hbm] * n,
        out_specs=(hbm,) * n,
        scratch_shapes=[pltpu.VMEM(a.shape, a.dtype) for a in arrays]
        + [pltpu.SemaphoreType.DMA((2, k)) for k in splits],
        compiler_params=pltpu.CompilerParams(vmem_limit_bytes=67043328),
    )(*arrays)


def fused_call(tok, placing, hot_ids, acts, grad_hidden, master, moment, second, slots):
    tensors = lax.axis_size("tensor")
    t, width = grad_hidden.shape
    hot, rows = master.shape
    chunks = rows // ROWS
    blocks = width // CB
    per = PER if blocks % PER == 0 else 1
    w = per * CB
    pieces = blocks // per
    n = chunks * pieces
    half = ROWS // 2
    bf16, f32 = jnp.bfloat16, jnp.float32
    dma = pltpu.SemaphoreType.DMA
    hbm = pl.BlockSpec(memory_space=pl.ANY)
    smem = pl.BlockSpec(memory_space=pltpu.SMEM)
    state = jax.ShapeDtypeStruct((hot, rows), f32)
    return pl.pallas_call(
        functools.partial(fused, (chunks, pieces, w, tensors, slots, width)),
        out_shape=(
            state, state, state,
            jax.ShapeDtypeStruct((hot, 2 * rows), bf16),
            jax.ShapeDtypeStruct((tensors * slots, rows, CB), bf16),
        ),
        in_specs=[smem, smem, pl.BlockSpec(memory_space=pltpu.VMEM)] + [hbm] * 5,
        out_specs=(hbm,) * 5,
        scratch_shapes=[
            pltpu.VMEM((rows // CB, GROUP, t, CB), bf16),
            pltpu.VMEM((pieces, t, w), bf16),
            pltpu.VMEM((2, GROUP * ROWS, t), bf16),
            pltpu.VMEM((pieces, hot, w), bf16),
            pltpu.VMEM((pieces, 8, w), f32),
            pltpu.VMEM((hot, CB), f32),
            pltpu.VMEM((3, hot, rows), f32),
            pltpu.VMEM((hot, rows), bf16),
            pltpu.VMEM((sum(LAGS) + 1, 2, GROUP, half, w), bf16),
            pltpu.VMEM((n, 2, 4, half, w), bf16),
            pltpu.VMEM((n, 2, 2, half, w), bf16),
            pltpu.VMEM((n, 2, half, w), bf16),
            pltpu.VMEM((blocks + 1, ROWS, CB), bf16),
            pltpu.VMEM((pieces, CB, w), bf16),
            pltpu.VMEM((chunks, tensors * slots, ROWS, CB), bf16),
            pltpu.VMEM((GROUP, 8, 128), f32),
            dma((rows // CB, GROUP)), dma((pieces,)), dma((3,)), dma((2, GROUP)),
            dma((n, 2)), dma((n, 2)), dma((n, 2)), dma((n, 2)), dma((n, 2)), dma((n, 2)),
            dma((chunks, tensors)), dma((chunks, tensors)), dma((3,)),
        ],
        compiler_params=pltpu.CompilerParams(
            collective_id=0, has_side_effects=True, vmem_limit_bytes=67043328
        ),
    )(tok, placing, hot_ids, acts, grad_hidden, master, moment, second)


def adam_update(g_hot, master_hot, moment_hot, second_hot):
    new_moment = 0.9 * moment_hot + 0.1 * g_hot
    new_second = 0.95 * second_hot + 0.05 * g_hot * g_hot
    bias_one = 1.0 - 0.9**4
    bias_two = 1.0 - 0.95**4
    new_master = master_hot - 0.02 * (new_moment / bias_one) / (
        jnp.sqrt(new_second / bias_two) + 1e-08
    )
    return (new_master, new_moment, new_second)


def shards(
    acts, grad_hidden, token_count, hot_ids, block_owner, master_hot, moment_hot, second_hot
):
    tok_slots = acts.shape[0]
    width = grad_hidden.shape[1]
    hot_count = hot_ids.shape[1]
    row_count = master_hot.shape[1]
    tensors = lax.axis_size("tensor")
    blocks = width // CB
    slots = max(2, (2 * blocks + tensors - 1) // tensors)
    if lax.axis_size("dp") == 4 and lax.axis_size("pipe") == 2 and row_count % CB == 0:
        owner = block_owner[:, 0]
        same = owner[:, None] == owner[None, :]
        index = lax.broadcasted_iota(jnp.int32, (blocks, blocks), 0)
        other = lax.broadcasted_iota(jnp.int32, (blocks, blocks), 1)
        slot = jnp.sum((same & (other < index)).astype(jnp.int32), axis=1)
        target = owner * slots + slot
        places = lax.broadcasted_iota(jnp.int32, (tensors * slots, blocks), 0)
        number = lax.broadcasted_iota(jnp.int32, (tensors * slots, blocks), 1)
        from_block = jnp.min(jnp.where(places == target[None, :], number, blocks), axis=1)
        results = fused_call(
            token_count, from_block, hot_ids.reshape(hot_count, 1), acts, grad_hidden,
            master_hot, moment_hot, second_hot, slots,
        )
        return hand_out_call(results, (1, 1, 1, 1, tensors))
    live = lax.broadcasted_iota(jnp.int32, (tok_slots, 1), 0) < token_count[0]
    masked = jnp.where(live, grad_hidden, jnp.zeros_like(grad_hidden))
    total = lax.psum(token_count.astype(jnp.float32)[0], ("dp", "pipe"))
    column = lax.broadcasted_iota(jnp.int32, (width, hot_count), 0)
    selector = column == hot_ids[0][None, :]
    hot_mask = jnp.any(selector, axis=1)
    contract = (((0,), (0,)), ((), ()))
    summed = lax.psum_scatter(
        lax.dot_general(acts, masked, contract, preferred_element_type=jnp.float32).astype(
            jnp.bfloat16
        ),
        ("dp", "pipe"),
        scatter_dimension=0,
        tiled=True,
    ).astype(jnp.float32)
    grad = summed / total
    g_hot = lax.dot_general(
        selector.astype(jnp.float32),
        grad,
        (((0,), (1,)), ((), ())),
        precision=lax.Precision.HIGHEST,
        preferred_element_type=jnp.float32,
    )
    cold = jnp.where(hot_mask[None, :], 0.0, grad).astype(jnp.bfloat16)
    new_master, new_moment, new_second = adam_update(g_hot, master_hot, moment_hot, second_hot)
    hot_weights = lax.all_gather(new_master.astype(jnp.bfloat16), "pipe", axis=1, tiled=True)
    owner = block_owner[:, 0]
    same = owner[:, None] == owner[None, :]
    index = lax.broadcasted_iota(jnp.int32, (blocks, blocks), 0)
    other = lax.broadcasted_iota(jnp.int32, (blocks, blocks), 1)
    slot = jnp.sum((same & (other < index)).astype(jnp.int32), axis=1)
    target = owner * slots + slot
    places = lax.broadcasted_iota(jnp.int32, (tensors * slots, blocks), 0)
    placing = (places == target[None, :]).astype(jnp.bfloat16)
    tiles = cold.reshape(row_count, blocks, CB)
    packed = jnp.einsum("pb,rbc->prc", placing, tiles, preferred_element_type=jnp.float32).astype(
        jnp.bfloat16
    )
    cold_sectioning = lax.all_to_all(packed, "tensor", split_axis=0, concat_axis=0, tiled=True)
    return (new_master, new_moment, new_second, hot_weights, cold_sectioning)


def solution(mesh):
    in_specs = (
        P(("dp", "pipe"), None),
        P(("dp", "pipe"), "tensor"),
        P(("dp", "pipe")),
        P("tensor", None),
        P("tensor", None),
        P("tensor", ("dp", "pipe")),
        P("tensor", ("dp", "pipe")),
        P("tensor", ("dp", "pipe")),
    )
    out_specs = (
        P("tensor", ("dp", "pipe")),
        P("tensor", ("dp", "pipe")),
        P("tensor", ("dp", "pipe")),
        P("tensor", "dp"),
        P("tensor", ("dp", "pipe"), None),
    )
    return jax.shard_map(shards, mesh=mesh, in_specs=in_specs, out_specs=out_specs, check_vma=False)
```

```python
import functools

import jax
import jax.numpy as jnp
from jax import lax
from jax.experimental import pallas as pl
from jax.experimental.pallas import tpu as pltpu
from jax.sharding import PartitionSpec as P

CB = 128
GROUP = 8
ROWS = 32
SUB = CB // ROWS
PER = 14
LAGS = (1, 2, 2)


def fused(
    sizes, tc_ref, place_ref, hid_ref, acts, gh, mst, mom, sec,
    mst_out, mom_out, sec_out, hw_out, cs_out,
    acts_v, gh_v, acts_t, select, keep, hot_acc, state, hw_v, slots_v,
    recv_a, recv_b, recv_c, tiles, sums, packed, count,
    acts_sem, gh_sem, state_sem, count_sem, send_a, land_a, send_b, land_b, send_c, land_c,
    z_send, z_land, hw_sem,
):
    chunks, pieces, w, tensors, slots, width = sizes
    half = ROWS // 2
    total_pieces = chunks * pieces
    ring = slots_v.shape[0]
    row_count = chunks * ROWS
    lag_b = LAGS[0]
    lag_c = lag_b + LAGS[1]
    lag_d = lag_c + LAGS[2]
    dp, tz, pp = lax.axis_index("dp"), lax.axis_index("tensor"), lax.axis_index("pipe")
    y, x = dp // 2, dp % 2

    def peer(qy, qx, qc):
        return (((y + qy) % 2) * 2 + (x + qx) % 2, tz, (pp + qc) % 2)

    def remote(src, dst, ssem, rsem, device):
        return pltpu.make_async_remote_copy(
            src_ref=src, dst_ref=dst, send_sem=ssem, recv_sem=rsem,
            device_id=device, device_id_type=pl.DeviceIdType.MESH,
        )

    def acts_copy(c, o):
        return pltpu.make_async_copy(
            acts.at[:, pl.ds(pl.multiple_of(o * row_count + c * CB, CB), CB)],
            acts_v.at[c, o], acts_sem.at[c, o],
        )

    def gh_copy(p):
        return pltpu.make_async_copy(
            gh.at[:, pl.ds(pl.multiple_of(p * w, CB), w)], gh_v.at[p], gh_sem.at[p]
        )

    state_in = [
        pltpu.make_async_copy(r, state.at[k], state_sem.at[k])
        for k, r in enumerate((mst, mom, sec))
    ]
    for o in range(GROUP):
        acts_copy(0, o).start()
    gh_copy(0).start()
    for p in range(1, pieces):
        gh_copy(p).start()
    for c in range(1, row_count // CB):
        for o in range(GROUP):
            acts_copy(c, o).start()
    for cp in state_in:
        cp.start()

    count[0] = jnp.full((8, 128), tc_ref[0], jnp.int32).astype(jnp.float32)
    barrier = pltpu.get_barrier_semaphore()
    for q in range(1, GROUP):
        pl.semaphore_signal(
            barrier, inc=1, device_id=peer(q // 4, (q // 2) % 2, q % 2),
            device_id_type=pl.DeviceIdType.MESH,
        )
    for d in range(1, tensors):
        pl.semaphore_signal(
            barrier, inc=1, device_id=(dp, (tz + d) % tensors, pp),
            device_id_type=pl.DeviceIdType.MESH,
        )
    pl.semaphore_wait(barrier, GROUP - 1 + tensors - 1)

    counts = [
        remote(
            count.at[0], count.at[q], count_sem.at[0, q], count_sem.at[1, q],
            peer(q // 4, (q // 2) % 2, q % 2),
        )
        for q in range(1, GROUP)
    ]
    for cp in counts:
        cp.start()

    def copy_a(i, h):
        return remote(
            slots_v.at[i % ring, h, pl.ds(4, 4)], recv_a.at[i, h],
            send_a.at[i, h], land_a.at[i, h], peer(0, 0, 1),
        )

    def copy_b(i, h):
        return remote(
            slots_v.at[i % ring, h, pl.ds(2, 2)], recv_b.at[i, h],
            send_b.at[i, h], land_b.at[i, h], peer(h, 1 - h, 0),
        )

    def copy_c(i, h):
        return remote(
            slots_v.at[i % ring, h, 1], recv_c.at[i, h],
            send_c.at[i, h], land_c.at[i, h], peer(1 - h, h, 0),
        )

    def z_copy(c, d):
        return remote(
            packed.at[c, pl.ds(((tz + d) % tensors) * slots, slots)],
            cs_out.at[pl.ds(tz * slots, slots), pl.ds(c * ROWS, ROWS)],
            z_send.at[c, d], z_land.at[c, d], (dp, (tz + d) % tensors, pp),
        )

    def z_own(c):
        return pltpu.make_async_copy(
            packed.at[c, pl.ds(tz * slots, slots)],
            cs_out.at[pl.ds(tz * slots, slots), pl.ds(c * ROWS, ROWS)],
            z_send.at[c, 0],
        )

    tok = acts_v.shape[2]
    live = lax.broadcasted_iota(jnp.int32, (tok, CB), 0) < tc_ref[0]
    hot_acc[...] = jnp.zeros_like(hot_acc)
    tiles[tiles.shape[0] - 1] = jnp.zeros((ROWS, CB), tiles.dtype)

    def multiply(i):
        c, p = i // pieces, i % pieces

        @pl.when((p == 0) & (c % SUB == 0))
        def _():
            for o in range(GROUP):
                acts_copy(c // SUB, o).wait()
            for q in range(GROUP):
                qc, q1, q0 = q // 4, (q // 2) % 2, q % 2
                o = ((y + q0) % 2) * 4 + ((x + q1) % 2) * 2 + (pp + qc) % 2
                v = jnp.where(live, acts_v[c // SUB, o].astype(jnp.float32), 0.0)
                v = v.T.astype(jnp.bfloat16)
                for u in range(SUB):
                    acts_t[u, pl.ds(q * ROWS, ROWS)] = v[u * ROWS : (u + 1) * ROWS]

        @pl.when(c == 0)
        def _():
            gh_copy(p).wait()

        r = jnp.dot(
            acts_t[c % SUB], gh_v[p], preferred_element_type=jnp.float32
        ).astype(jnp.bfloat16)
        for q in range(GROUP):
            k, a, b = q // 4, q % 2, (q // 2) % 2
            slots_v[i % ring, 0, q] = r[q * ROWS : q * ROWS + half]
            slots_v[i % ring, 1, k * 4 + a * 2 + b] = r[q * ROWS + half : (q + 1) * ROWS]
        for h in range(2):
            copy_a(i, h).start()

    def prepare():
        for p in range(pieces):
            column = lax.broadcasted_iota(jnp.int32, (select.shape[1], w), 1) + p * w
            hit = (column == hid_ref[...]).astype(jnp.float32)
            select[p] = hit.astype(jnp.bfloat16)
            keep[p] = jnp.broadcast_to(1.0 - jnp.max(hit, axis=0, keepdims=True), (8, w))
        for cp in counts:
            cp.wait()
        for cp in state_in:
            cp.wait()

    f32 = jnp.float32

    def step_b(i):
        for h in range(2):
            copy_a(i, h).wait()
            for k in (2, 3, 0, 1):
                slots_v[i % ring, h, k] = (
                    slots_v[i % ring, h, k].astype(f32) + recv_a[i, h, k].astype(f32)
                ).astype(jnp.bfloat16)
            copy_b(i, h).start()

    def step_c(i):
        for h in range(2):
            copy_b(i, h).wait()
            for k in (1, 0):
                slots_v[i % ring, h, k] = (
                    slots_v[i % ring, h, k].astype(f32) + recv_b[i, h, k].astype(f32)
                ).astype(jnp.bfloat16)
            copy_c(i, h).start()

    def step_d(i):
        c, p = i // pieces, i % pieces
        total = count[0]
        for q in range(1, GROUP):
            total = total + count[q]
        total = total[0:1, 0:1]
        for h in range(2):
            copy_c(i, h).wait()
            s = slots_v[i % ring, h, 0].astype(f32) + recv_c[i, h].astype(f32)
            cold = jnp.where(keep[p][0:1] > 0.5, s / total, 0.0).astype(jnp.bfloat16)
            for b in range(w // CB):
                tiles[p * (w // CB) + b, pl.ds(h * half, half)] = cold[:, b * CB : (b + 1) * CB]
            sums[p, pl.ds((c % SUB) * ROWS + h * half, half)] = s.astype(jnp.bfloat16)

        @pl.when(c % SUB == SUB - 1)
        def _():
            g = lax.dot_general(
                select[p], sums[p], (((1,), (1,)), ((), ())), preferred_element_type=f32
            )
            hot_acc[...] = jnp.where(p == 0, 0.0, hot_acc[...]) + g

        @pl.when(p == pieces - 1)
        def _():
            def place(k, carry):
                packed[c, k] = tiles[place_ref[k]]
                return carry

            lax.fori_loop(0, tensors * slots, place, 0)
            for d in range(tensors - 1, 0, -1):
                z_copy(c, d).start()
            z_own(c).start()

        @pl.when((p == pieces - 1) & (c % SUB == SUB - 1))
        def _():
            cols = pl.ds(pl.multiple_of((c // SUB) * CB, CB), CB)
            out = adam_update(
                hot_acc[...] / total, state[0, :, cols], state[1, :, cols], state[2, :, cols]
            )
            for k in range(3):
                state[k, :, cols] = out[k]
            hw_v[:, cols] = out[0].astype(jnp.bfloat16)

    def body(i, carry):
        @pl.when(i < total_pieces)
        def _():
            multiply(i)

        @pl.when(i == 1)
        def _():
            prepare()

        @pl.when((i >= lag_d) & (i < total_pieces + lag_d))
        def _():
            step_d(i - lag_d)

        @pl.when((i >= lag_c) & (i < total_pieces + lag_c))
        def _():
            step_c(i - lag_c)

        @pl.when((i >= lag_b) & (i < total_pieces + lag_b))
        def _():
            step_b(i - lag_b)

        return carry

    lax.fori_loop(0, total_pieces + lag_d, body, 0)

    mine = hw_out.at[:, pl.ds(pl.multiple_of(pp * row_count, CB), row_count)]
    swap = remote(hw_v, mine, hw_sem.at[0], hw_sem.at[1], peer(0, 0, 1))
    swap.start()
    outs = [
        pltpu.make_async_copy(state.at[k], r, state_sem.at[k])
        for k, r in enumerate((mst_out, mom_out, sec_out))
    ]
    outs.append(pltpu.make_async_copy(hw_v, mine, hw_sem.at[2]))
    for cp in outs:
        cp.start()
    for cp in outs:
        cp.wait()
    swap.wait()
    for c in range(chunks):
        z_own(c).wait()
        for d in range(tensors - 1, 0, -1):
            z_copy(c, d).wait()


def hand_out(refs, outs, bufs, sems, splits):
    jobs = []
    for k in range(len(splits)):
        size = bufs[k].shape[0] // splits[k]
        for j in range(splits[k]):
            part = pl.ds(j * size, size)
            jobs.append((
                pltpu.make_async_copy(refs[k].at[part], bufs[k].at[part], sems[k].at[0, j]),
                pltpu.make_async_copy(bufs[k].at[part], outs[k].at[part], sems[k].at[1, j]),
            ))
    for load, _ in jobs:
        load.start()
    for load, store in jobs:
        load.wait()
        store.start()
    for _, store in jobs:
        store.wait()


def hand_out_call(arrays, splits):
    n = len(arrays)
    hbm = pl.BlockSpec(memory_space=pl.ANY)

    def kernel(*refs):
        hand_out(refs[:n], refs[n : 2 * n], refs[2 * n : 3 * n], refs[3 * n :], splits)

    return pl.pallas_call(
        kernel,
        out_shape=tuple(jax.ShapeDtypeStruct(a.shape, a.dtype) for a in arrays),
        in_specs=[hbm] * n,
        out_specs=(hbm,) * n,
        scratch_shapes=[pltpu.VMEM(a.shape, a.dtype) for a in arrays]
        + [pltpu.SemaphoreType.DMA((2, k)) for k in splits],
        compiler_params=pltpu.CompilerParams(vmem_limit_bytes=67043328),
    )(*arrays)


def fused_call(tok, placing, hot_ids, acts, grad_hidden, master, moment, second, slots):
    tensors = lax.axis_size("tensor")
    t, width = grad_hidden.shape
    hot, rows = master.shape
    chunks = rows // ROWS
    blocks = width // CB
    per = PER if blocks % PER == 0 else 1
    w = per * CB
    pieces = blocks // per
    n = chunks * pieces
    half = ROWS // 2
    bf16, f32 = jnp.bfloat16, jnp.float32
    dma = pltpu.SemaphoreType.DMA
    hbm = pl.BlockSpec(memory_space=pl.ANY)
    smem = pl.BlockSpec(memory_space=pltpu.SMEM)
    state = jax.ShapeDtypeStruct((hot, rows), f32)
    return pl.pallas_call(
        functools.partial(fused, (chunks, pieces, w, tensors, slots, width)),
        out_shape=(
            state, state, state,
            jax.ShapeDtypeStruct((hot, 2 * rows), bf16),
            jax.ShapeDtypeStruct((tensors * slots, rows, CB), bf16),
        ),
        in_specs=[smem, smem, pl.BlockSpec(memory_space=pltpu.VMEM)] + [hbm] * 5,
        out_specs=(hbm,) * 5,
        scratch_shapes=[
            pltpu.VMEM((rows // CB, GROUP, t, CB), bf16),
            pltpu.VMEM((pieces, t, w), bf16),
            pltpu.VMEM((SUB, GROUP * ROWS, t), bf16),
            pltpu.VMEM((pieces, hot, w), bf16),
            pltpu.VMEM((pieces, 8, w), f32),
            pltpu.VMEM((hot, CB), f32),
            pltpu.VMEM((3, hot, rows), f32),
            pltpu.VMEM((hot, rows), bf16),
            pltpu.VMEM((sum(LAGS) + 1, 2, GROUP, half, w), bf16),
            pltpu.VMEM((n, 2, 4, half, w), bf16),
            pltpu.VMEM((n, 2, 2, half, w), bf16),
            pltpu.VMEM((n, 2, half, w), bf16),
            pltpu.VMEM((blocks + 1, ROWS, CB), bf16),
            pltpu.VMEM((pieces, CB, w), bf16),
            pltpu.VMEM((chunks, tensors * slots, ROWS, CB), bf16),
            pltpu.VMEM((GROUP, 8, 128), f32),
            dma((rows // CB, GROUP)), dma((pieces,)), dma((3,)), dma((2, GROUP)),
            dma((n, 2)), dma((n, 2)), dma((n, 2)), dma((n, 2)), dma((n, 2)), dma((n, 2)),
            dma((chunks, tensors)), dma((chunks, tensors)), dma((3,)),
        ],
        compiler_params=pltpu.CompilerParams(
            collective_id=0, has_side_effects=True, vmem_limit_bytes=67043328
        ),
    )(tok, placing, hot_ids, acts, grad_hidden, master, moment, second)


def adam_update(g_hot, master_hot, moment_hot, second_hot):
    new_moment = 0.9 * moment_hot + 0.1 * g_hot
    new_second = 0.95 * second_hot + 0.05 * g_hot * g_hot
    bias_one = 1.0 - 0.9**4
    bias_two = 1.0 - 0.95**4
    new_master = master_hot - 0.02 * (new_moment / bias_one) / (
        jnp.sqrt(new_second / bias_two) + 1e-08
    )
    return (new_master, new_moment, new_second)


def shards(
    acts, grad_hidden, token_count, hot_ids, block_owner, master_hot, moment_hot, second_hot
):
    tok_slots = acts.shape[0]
    width = grad_hidden.shape[1]
    hot_count = hot_ids.shape[1]
    row_count = master_hot.shape[1]
    tensors = lax.axis_size("tensor")
    blocks = width // CB
    slots = max(2, (2 * blocks + tensors - 1) // tensors)
    if lax.axis_size("dp") == 4 and lax.axis_size("pipe") == 2 and row_count % CB == 0:
        owner = block_owner[:, 0]
        same = owner[:, None] == owner[None, :]
        index = lax.broadcasted_iota(jnp.int32, (blocks, blocks), 0)
        other = lax.broadcasted_iota(jnp.int32, (blocks, blocks), 1)
        slot = jnp.sum((same & (other < index)).astype(jnp.int32), axis=1)
        target = owner * slots + slot
        places = lax.broadcasted_iota(jnp.int32, (tensors * slots, blocks), 0)
        number = lax.broadcasted_iota(jnp.int32, (tensors * slots, blocks), 1)
        from_block = jnp.min(jnp.where(places == target[None, :], number, blocks), axis=1)
        results = fused_call(
            token_count, from_block, hot_ids.reshape(hot_count, 1), acts, grad_hidden,
            master_hot, moment_hot, second_hot, slots,
        )
        return hand_out_call(results, (1, 1, 1, 1, tensors))
    live = lax.broadcasted_iota(jnp.int32, (tok_slots, 1), 0) < token_count[0]
    masked = jnp.where(live, grad_hidden, jnp.zeros_like(grad_hidden))
    total = lax.psum(token_count.astype(jnp.float32)[0], ("dp", "pipe"))
    column = lax.broadcasted_iota(jnp.int32, (width, hot_count), 0)
    selector = column == hot_ids[0][None, :]
    hot_mask = jnp.any(selector, axis=1)
    contract = (((0,), (0,)), ((), ()))
    summed = lax.psum_scatter(
        lax.dot_general(acts, masked, contract, preferred_element_type=jnp.float32).astype(
            jnp.bfloat16
        ),
        ("dp", "pipe"),
        scatter_dimension=0,
        tiled=True,
    ).astype(jnp.float32)
    grad = summed / total
    g_hot = lax.dot_general(
        selector.astype(jnp.float32),
        grad,
        (((0,), (1,)), ((), ())),
        precision=lax.Precision.HIGHEST,
        preferred_element_type=jnp.float32,
    )
    cold = jnp.where(hot_mask[None, :], 0.0, grad).astype(jnp.bfloat16)
    new_master, new_moment, new_second = adam_update(g_hot, master_hot, moment_hot, second_hot)
    hot_weights = lax.all_gather(new_master.astype(jnp.bfloat16), "pipe", axis=1, tiled=True)
    owner = block_owner[:, 0]
    same = owner[:, None] == owner[None, :]
    index = lax.broadcasted_iota(jnp.int32, (blocks, blocks), 0)
    other = lax.broadcasted_iota(jnp.int32, (blocks, blocks), 1)
    slot = jnp.sum((same & (other < index)).astype(jnp.int32), axis=1)
    target = owner * slots + slot
    places = lax.broadcasted_iota(jnp.int32, (tensors * slots, blocks), 0)
    placing = (places == target[None, :]).astype(jnp.bfloat16)
    tiles = cold.reshape(row_count, blocks, CB)
    packed = jnp.einsum("pb,rbc->prc", placing, tiles, preferred_element_type=jnp.float32).astype(
        jnp.bfloat16
    )
    cold_sectioning = lax.all_to_all(packed, "tensor", split_axis=0, concat_axis=0, tiled=True)
    return (new_master, new_moment, new_second, hot_weights, cold_sectioning)


def solution(mesh):
    in_specs = (
        P(("dp", "pipe"), None),
        P(("dp", "pipe"), "tensor"),
        P(("dp", "pipe")),
        P("tensor", None),
        P("tensor", None),
        P("tensor", ("dp", "pipe")),
        P("tensor", ("dp", "pipe")),
        P("tensor", ("dp", "pipe")),
    )
    out_specs = (
        P("tensor", ("dp", "pipe")),
        P("tensor", ("dp", "pipe")),
        P("tensor", ("dp", "pipe")),
        P("tensor", "dp"),
        P("tensor", ("dp", "pipe"), None),
    )
    return jax.shard_map(shards, mesh=mesh, in_specs=in_specs, out_specs=out_specs, check_vma=False)
```
